32 devices in a mesh: dp: 4 (over y, core), tm: 8 (over z, x).
Axes of the slice: x: 2, y: 2, z: 4, core: 2. Of those that a mesh axis runs over, the one named last changes fastest.
Arguments:
- features: bfloat16 [4, 16, 48, 48, 128], P('dp', 'tm'), may hold values from -6 to 6
- frame_counts: int32 [4, 6], P('dp'), may hold values from 1 to 8, 16 in all within a row
- conv1_weight: bfloat16 [3, 3, 3, 128, 128], replicated, may hold values from -0.109375 to 0.109375
- conv1_bias: float32 [128], replicated, may hold values from -3 to 3
- shrink_weight: bfloat16 [512, 128], replicated, may hold values from -0.25 to 0.25
- shrink_bias: float32 [128], replicated, may hold values from -3 to 3
- conv2_weight: bfloat16 [3, 3, 3, 128, 128], replicated, may hold values from -0.109375 to 0.109375
- conv2_bias: float32 [128], replicated, may hold values from -3 to 3
- embed_weight: bfloat16 [512, 1152], replicated, may hold values from -0.25 to 0.25
- embed_bias: float32 [1152], replicated, may hold values from -3 to 3
- bucket_table: float32 [8, 1152], replicated, may hold values from -5 to 5
- bucket_ids: int32 [4, 2304], P('dp', 'tm'), may hold values from 0 to 7
- dest_owner: int32 [4, 2304], P('dp', 'tm'), may hold values from 0 to 3, as said below
- dest_offset: int32 [4, 2304], P('dp', 'tm'), may hold values from 0 to 575, as said below
Outputs:
- packs: bfloat16 [4, 4608, 1152], P('dp', 'tm')
The draws below stay inside these ranges and needn't reach their ends.
Inputs may be any that keep to these rules, and one draw needn't show every extreme that they name: `dest_owner`: among the 288 rows of one device (r // 288 fixed) each owner is named at most 144 times; for each index of tm one owner is named exactly 144 times by every device of dp. `dest_offset`: the rows that share an owner and a value of r // 288 have distinct offsets.
All inputs are finite; a program needn't handle non-finite values.
Results may differ from the reference program's by a relative error of at most 0.0056.
Values may be sent and summed in bfloat16 or wider, within the bound.
A program may use at most 128 MiB of HBM per device.

```python
import math
import jax
import jax.numpy as jnp
import numpy as np
from jax import lax

C = 128
LAT = 1152
TAPS = 3
SIDE = 48
VIDS = 6
NB = 8
GROUPS = 4
FRAMES = 16
ROWS_DEV = 288
LROWS = 2304
CAP = 144
PACK = 576
SLOTS = 4608


def route_tables(key):
    column_count = LROWS // ROWS_DEV
    others = (GROUPS - 1) * CAP
    preference_key = jax.random.fold_in(key, 11)
    choose_key = jax.random.fold_in(key, 12)
    shuffle_key = jax.random.fold_in(key, 13)
    slot_key = jax.random.fold_in(key, 14)
    favoured = jax.random.randint(preference_key, (column_count,), 0, GROUPS).astype(jnp.int32)
    scores = jax.random.randint(choose_key, (GROUPS, column_count, others), 0, 1 << 20) * others + jnp.arange(others, dtype=jnp.int32)
    chosen = jnp.argsort(scores, axis=-1)[..., :ROWS_DEV - CAP].astype(jnp.int32)
    owners_rest = chosen // CAP
    favour_wide = favoured[None, :, None]
    owners_rest = owners_rest + (owners_rest >= favour_wide).astype(jnp.int32)
    owners = jnp.concatenate([jnp.broadcast_to(favour_wide, (GROUPS, column_count, CAP)), owners_rest], axis=-1)
    shuffle_scores = jax.random.randint(shuffle_key, (GROUPS, column_count, ROWS_DEV), 0, 1 << 20) * ROWS_DEV + jnp.arange(ROWS_DEV, dtype=jnp.int32)
    owners = jnp.take_along_axis(owners, jnp.argsort(shuffle_scores, axis=-1), axis=-1).astype(jnp.int32)
    match_flags = (owners[..., None] == jnp.arange(GROUPS, dtype=jnp.int32)).astype(jnp.int32)
    position = jnp.sum((jnp.cumsum(match_flags, axis=2) - 1) * match_flags, axis=-1)
    slot_scores = jax.random.randint(slot_key, (GROUPS, column_count, PACK), 0, 1 << 20) * PACK + jnp.arange(PACK, dtype=jnp.int32)
    slot_table = jnp.argsort(slot_scores, axis=-1).astype(jnp.int32)
    sources = jnp.arange(GROUPS, dtype=jnp.int32)[:, None, None]
    columns = jnp.arange(column_count, dtype=jnp.int32)[None, :, None]
    offsets = slot_table[owners, columns, sources * CAP + position]
    return (owners.reshape(GROUPS, LROWS), offsets.reshape(GROUPS, LROWS).astype(jnp.int32))


def draw_dest_owner(key, part):
    return route_tables(jax.random.fold_in(key, 7))[0]


def draw_dest_offset(key, part):
    return route_tables(jax.random.fold_in(key, 7))[1]


def with_ends(result, rng, least, largest):
    spot = [jax.random.randint(jax.random.fold_in(rng, axis), (), 0, length) for axis, length in enumerate(result.shape)]
    widest = result.shape.index(max(result.shape))
    next_to = spot[:widest] + [(spot[widest] + 1) % result.shape[widest]] + spot[widest + 1:]
    return result.at[tuple(spot)].set(least).at[tuple(next_to)].set(largest)


def level_of(own_key, dims, split, least, top_value):
    loudness = 1.0
    for axis_at, blocks in split:
        steps = jax.random.uniform(jax.random.fold_in(jax.random.fold_in(own_key, 6), axis_at), (blocks,), jnp.float32, least / len(split), top_value / len(split))
        loudness = loudness * jnp.repeat(jnp.exp(steps), dims[axis_at] // blocks).reshape((-1,) + (1,) * (len(dims) - 1 - axis_at))
    return loudness


def split_up(number_of, total, limit, skew):
    weights = [(1 << 20) // math.isqrt(standing ** skew) + 1 for standing in range(2, number_of + 1)]
    surplus, holding = total - limit - (number_of - 1), [1] * (number_of - 1)
    while surplus > 0:
        movable = [i for i in range(number_of - 1) if holding[i] < limit]
        whole, remaining = sum([weights[i] for i in movable]), surplus
        for i in movable:
            more = min(limit - holding[i], max(1, remaining * weights[i] // whole), surplus)
            holding[i] = holding[i] + more
            surplus = surplus - more
    return np.array([limit] + holding)


def ragged_sizes(own_key, number_of, total, reach, lean):
    if number_of == 2:
        one = jax.random.randint(own_key, (), max(1, total - reach), min(reach, total - 1) + 1)
        return jnp.stack([one, total - one])
    tallies = jnp.asarray(split_up(number_of, total, reach, lean), jnp.int32)
    couples = (number_of - 1) // 2
    source_of, receiver = tallies[1:1 + 2 * couples:2], tallies[2:2 + 2 * couples:2]
    margin = jnp.minimum(source_of - 1, reach - receiver)
    moved = jax.random.randint(jax.random.fold_in(own_key, 1), (couples,), 0, 1 << 20) % (margin + 1)
    tallies = tallies.at[1:1 + 2 * couples:2].set(source_of - moved).at[2:2 + 2 * couples:2].set(receiver + moved)
    return tallies[jax.random.permutation(jax.random.fold_in(own_key, 2), number_of)]


def gaussian(rng, extent, scale, most, cuts=(), kind=jnp.bfloat16):
    loudness = level_of(rng, extent, cuts, -0.22, 0.18) if cuts else 1.0
    values = jax.random.normal(rng, extent, jnp.float32) * scale * loudness
    return jnp.minimum(jnp.maximum(values, -most), most).astype(kind)


def setup_inputs(seed: int = 0) -> dict:
    keys = jax.random.split(jax.random.key(seed), 15)
    return {
        "features": gaussian(keys[0], (GROUPS, FRAMES, SIDE, SIDE, C), 1.0, 6.0, ((0, 4), (1, 8))),
        "frame_counts": jax.vmap(lambda own: ragged_sizes(own, VIDS, FRAMES, FRAMES // 2, 2))(jax.random.split(keys[1], GROUPS)).reshape((GROUPS, VIDS)).astype(jnp.int32),
        "conv1_weight": gaussian(keys[2], (TAPS, 3, 3, C, C), (TAPS * 9 * C) ** -0.5, 0.109375),
        "conv1_bias": gaussian(keys[3], (C,), 0.5, 3.0, (), jnp.float32),
        "shrink_weight": gaussian(keys[4], (4 * C, C), (4 * C) ** -0.5, 0.25),
        "shrink_bias": gaussian(keys[5], (C,), 0.5, 3.0, (), jnp.float32),
        "conv2_weight": gaussian(keys[6], (TAPS, 3, 3, C, C), (TAPS * 9 * C) ** -0.5, 0.109375),
        "conv2_bias": gaussian(keys[7], (C,), 0.5, 3.0, (), jnp.float32),
        "embed_weight": gaussian(keys[8], (4 * C, LAT), (4 * C) ** -0.5, 0.25),
        "embed_bias": gaussian(keys[9], (LAT,), 0.5, 3.0, (), jnp.float32),
        "bucket_table": gaussian(keys[10], (NB, LAT), 1.0, 5.0, (), jnp.float32),
        "bucket_ids": with_ends(jax.random.randint(keys[11], (GROUPS, LROWS), 0, NB), jax.random.fold_in(keys[11], 1), 0, NB - 1).astype(jnp.int32),
        "dest_owner": draw_dest_owner(jax.random.fold_in(keys[14], 71), 0),
        "dest_offset": draw_dest_offset(jax.random.fold_in(keys[14], 71), 0),
    }


def frame_masks(counts, first_frame, length):
    frames = first_frame + jnp.arange(length, dtype=jnp.int32)
    bounds = jnp.cumsum(counts).astype(jnp.int32)

    def segment(moments):
        return jnp.sum((moments[:, None] >= bounds[None, :]).astype(jnp.int32), axis=1)

    current = segment(frames)
    columns = []
    for distance in (2, 1):
        earlier = frames - distance
        columns.append(((earlier >= 0) & (segment(earlier) == current)).astype(jnp.float32))
    return jnp.stack(columns, axis=1)


def causal_conv(window, valid, kernel, conv_bias):
    outputs = valid.shape[0]
    side = window.shape[1]
    channels = window.shape[3]
    nothing = jnp.zeros((), window.dtype)
    oldest = jnp.where(valid[:, 0, None, None, None] > 0, window[0:outputs], nothing)
    middle = jnp.where(valid[:, 1, None, None, None] > 0, window[1:outputs + 1], nothing)
    stacked = jnp.concatenate([oldest, middle, window[2:outputs + 2]], axis=-1)
    padded = jnp.pad(stacked, ((0, 0), (1, 1), (1, 1), (0, 0)))
    taps_all = kernel.transpose(1, 2, 0, 3, 4).reshape(3, 3, 3 * channels, channels)
    total = jnp.zeros((outputs * side * side, channels), jnp.float32)
    for row_step in range(3):
        for col_step in range(3):
            piece = padded[:, row_step:row_step + side, col_step:col_step + side, :].reshape(-1, 3 * channels)
            total = total + jnp.dot(piece, taps_all[row_step, col_step], preferred_element_type=jnp.float32)
    return total.reshape(outputs, side, side, channels) + conv_bias


def fold_blocks(receptive_field):
    frame_total = receptive_field.shape[0]
    side = receptive_field.shape[1]
    channels = receptive_field.shape[3]
    blocks = receptive_field.reshape(frame_total, side // 2, 2, side // 2, 2, channels).transpose(0, 1, 3, 2, 4, 5)
    return blocks.reshape(frame_total, side // 2, side // 2, 4 * channels)


def residual_section(window, valid, kernel, conv_bias, inputs):
    return (inputs.astype(jnp.float32) + jax.nn.silu(causal_conv(window, valid, kernel, conv_bias))).astype(jnp.bfloat16)


def spatial_shrink(receptive_field, shrink_weight, shrink_bias):
    folded = fold_blocks(receptive_field)
    shape_out = folded.shape[:3] + (shrink_weight.shape[1],)
    mixed = jnp.dot(folded.reshape(-1, folded.shape[3]), shrink_weight, preferred_element_type=jnp.float32) + shrink_bias
    return mixed.astype(jnp.bfloat16).reshape(shape_out)


def reference(features, frame_counts, conv1_weight, conv1_bias, shrink_weight, shrink_bias, conv2_weight, conv2_bias, embed_weight, embed_bias, bucket_table, bucket_ids, dest_owner, dest_offset):
    def one_row(inputs):
        slab, counts, buckets = inputs
        valid = frame_masks(counts, jnp.int32(0), FRAMES)
        padding = jnp.zeros((2,) + slab.shape[1:], slab.dtype)
        section_first = residual_section(jnp.concatenate([padding, slab], axis=0), valid, conv1_weight, conv1_bias, slab)
        reduced_result = spatial_shrink(section_first, shrink_weight, shrink_bias)
        padding_two = jnp.zeros((2,) + reduced_result.shape[1:], reduced_result.dtype)
        section_two = residual_section(jnp.concatenate([padding_two, reduced_result], axis=0), valid, conv2_weight, conv2_bias, reduced_result)
        patches = fold_blocks(section_two).reshape(-1, 4 * section_two.shape[3])
        latent = jnp.dot(patches, embed_weight, preferred_element_type=jnp.float32) + embed_bias + bucket_table[buckets]
        return latent.astype(jnp.bfloat16)

    latents = lax.map(one_row, (features, frame_counts, bucket_ids))
    column_count = LROWS // ROWS_DEV
    columns = jnp.arange(LROWS, dtype=jnp.int32) // ROWS_DEV
    flat = dest_owner * (column_count * PACK) + columns[None, :] * PACK + dest_offset
    packs = jnp.zeros((GROUPS * column_count * PACK, LAT), jnp.bfloat16)
    packs = packs.at[flat.reshape(-1)].set(latents.reshape(-1, LAT))
    return packs.reshape(GROUPS, SLOTS, LAT)
```

```python
import functools
import jax
import jax.numpy as jnp
from jax import lax
from jax.experimental import pallas as pl
from jax.experimental.pallas import tpu as pltpu
from jax.sharding import PartitionSpec as P

MESH = pl.DeviceIdType.MESH
F32 = jnp.float32
BF16 = jnp.bfloat16
RED = ((0, 7), (7, 6), (13, 6), (19, 5))
FEAT = ((0, 15), (15, 12), (27, 12), (39, 9))
PIECES = 4
PAD = 8


def silu(v):
    return v / (1.0 + jnp.exp(-v))


def live_factors(counts_ref, first, videos):
    def segment(moment):
        total = jnp.int32(0)
        bound = jnp.int32(0)
        for i in range(videos):
            bound = bound + counts_ref[0, i]
            total = total + jnp.where(moment >= bound, 1, 0)
        return total

    seg = {d: segment(first + d) for d in (-2, -1, 0, 1)}

    def live(frame, distance):
        same = jnp.where(seg[frame] == seg[frame - distance], 1.0, 0.0)
        there = jnp.where(first + frame - distance >= 0, 1.0, 0.0)
        return (same * there).astype(F32)

    return live


def body(
    rows,
    pack,
    n_tm,
    n_dp,
    videos,
    feat,
    counts,
    w1,
    b1,
    sw,
    sb,
    w2,
    b2,
    bucket,
    owner,
    offset,
    patches_out,
    meta_out,
    xv,
    pv,
    p1,
    p2,
    wm1,
    wm2,
    acc,
    rsend,
    rrecv,
    fs,
    stage,
    psend,
    meta,
    local_sem,
    fsend_sem,
    frecv_sem,
    rsend_sem,
    rrecv_sem,
    psend_sem,
    precv_sem,
    msend_sem,
    mrecv_sem,
    own_sem,
):
    dp = lax.axis_index("dp")
    tm = lax.axis_index("tm")
    has_next = tm < n_tm - 1
    has_prev = tm > 0
    nxt = lax.rem(tm + 1, n_tm)
    prv = lax.rem(tm + n_tm - 1, n_tm)

    load = pltpu.make_async_copy(feat.at[0], xv, local_sem)
    load.start()

    barrier = pltpu.get_barrier_semaphore()

    @pl.when(has_next)
    def _():
        pl.semaphore_signal(barrier, inc=1, device_id=(dp, nxt), device_id_type=MESH)

    @pl.when(has_prev)
    def _():
        pl.semaphore_signal(barrier, inc=1, device_id=(dp, prv), device_id_type=MESH)

    for k in range(1, n_dp):
        pl.semaphore_signal(
            barrier, inc=1, device_id=(lax.rem(dp + k, n_dp), tm), device_id_type=MESH
        )

    beside = has_next.astype(jnp.int32) + has_prev.astype(jnp.int32)
    pl.semaphore_wait(barrier, n_dp - 1 + beside)

    def feat_copy(b):
        y0, n = FEAT[b]
        return pltpu.make_async_remote_copy(
            src_ref=feat.at[0, :, pl.ds(y0, n)],
            dst_ref=pv.at[:, pl.ds(y0, n)],
            send_sem=fsend_sem.at[b],
            recv_sem=frecv_sem.at[b],
            device_id=(dp, nxt),
            device_id_type=MESH,
        )

    def red_copy(b):
        n = 2 * RED[b][1] * 24
        return pltpu.make_async_remote_copy(
            src_ref=rsend.at[b, pl.ds(0, n)],
            dst_ref=rrecv.at[b, pl.ds(0, n)],
            send_sem=rsend_sem.at[b],
            recv_sem=rrecv_sem.at[b],
            device_id=(dp, nxt),
            device_id_type=MESH,
        )

    def patch_copy(b, k):
        return pltpu.make_async_remote_copy(
            src_ref=psend.at[b],
            dst_ref=patches_out.at[dp, b],
            send_sem=psend_sem.at[b, k],
            recv_sem=precv_sem.at[b, k],
            device_id=(lax.rem(dp + k, n_dp), tm),
            device_id_type=MESH,
        )

    def patch_own(b):
        return pltpu.make_async_copy(psend.at[b], patches_out.at[dp, b], own_sem.at[b])

    def meta_copy(k):
        return pltpu.make_async_remote_copy(
            src_ref=meta,
            dst_ref=meta_out.at[dp],
            send_sem=msend_sem.at[k],
            recv_sem=mrecv_sem.at[k],
            device_id=(lax.rem(dp + k, n_dp), tm),
            device_id_type=MESH,
        )

    def meta_own():
        return pltpu.make_async_copy(meta, meta_out.at[dp], own_sem.at[PIECES])

    @pl.when(has_next)
    def _():
        for b in range(PIECES):
            feat_copy(b).start()

    p1[...] = jnp.zeros(p1.shape, F32)
    p2[...] = jnp.zeros(p2.shape, F32)
    stage[...] = jnp.zeros(stage.shape, F32)

    @pl.when(tm == 0)
    def _():
        rrecv[...] = jnp.zeros(rrecv.shape, BF16)

    half = rows // 2
    quarter = half // PIECES
    width = meta.shape[1]
    block = width // PIECES
    row_at = lax.broadcasted_iota(jnp.int32, (rows, width), 0)
    col_at = lax.broadcasted_iota(jnp.int32, (rows, width), 1)
    order = jnp.zeros((rows, width), F32)
    for b in range(PIECES):
        for f in range(2):
            c0 = b * block + f * quarter
            hit = (
                (col_at - row_at == c0 - (f * half + b * quarter))
                & (col_at >= c0)
                & (col_at < c0 + quarter)
            )
            order = order + jnp.where(hit, 1.0, 0.0)
    code = (owner[...] * pack + offset[...] + 1).astype(F32)
    table = jnp.concatenate(
        [code, bucket[...].astype(F32), jnp.zeros((6, rows), F32)], axis=0
    )
    meta[...] = jnp.dot(
        table, order, precision=lax.Precision.HIGHEST, preferred_element_type=F32
    )
    meta_own().start()
    for k in range(1, n_dp):
        meta_copy(k).start()

    live = live_factors(counts, tm * 2, videos)
    for w, wm in ((w1, wm1), (w2, wm2)):
        wm[0, :, 0:128] = w[0] * live(0, 2).astype(BF16)
        wm[1, :, 0:128] = w[1] * live(0, 1).astype(BF16)
        wm[1, :, 128:256] = w[0] * live(1, 2).astype(BF16)
        wm[2, :, 0:128] = w[2]
        wm[2, :, 128:256] = w[1] * live(1, 1).astype(BF16)

    def field1(s, y0, n, parity):
        parts = []
        for dy in range(3):
            for dx in range(3):
                v = p1[s, y0 + dy : y0 + dy + n, pl.ds(PAD + parity + dx - 1, 24, stride=2), :]
                parts.append(v.reshape(n * 24, 128).astype(BF16))
        return jnp.concatenate(parts, axis=1)

    def field2(s, y0, n):
        parts = []
        for dy in range(3):
            for dx in range(3):
                v = p2[s, y0 + dy : y0 + dy + n, PAD + dx - 1 : PAD + dx + 23, :]
                parts.append(v.reshape(n * 24, 128).astype(BF16))
        return jnp.concatenate(parts, axis=1)

    def mm(a, w):
        return jnp.dot(a, w, preferred_element_type=F32)

    load.wait()
    for f in range(2):
        p1[2 + f, 1:49, PAD : PAD + 48, :] = xv[f].astype(F32)

    for b in range(PIECES):
        y0, n = 2 * RED[b][0], 2 * RED[b][1]
        for parity in range(2):
            both = mm(field1(2, y0, n, parity), wm1[2])
            last = mm(field1(3, y0, n, parity), w1[2])
            acc[0, parity, y0 * 24 : (y0 + n) * 24, :] = both[:, 0:128]
            acc[1, parity, y0 * 24 : (y0 + n) * 24, :] = both[:, 128:256] + last

    def section_one(b):
        f0, fn = FEAT[b]

        @pl.when(has_prev)
        def _():
            feat_copy(b).wait_recv()
            for f in range(2):
                p1[f, 1 + f0 : 1 + f0 + fn, PAD : PAD + 48, :] = pv[f, f0 : f0 + fn].astype(F32)

        y0, n = 2 * RED[b][0], 2 * RED[b][1]
        sides = []
        for parity in range(2):
            both = mm(field1(1, y0, n, parity), wm1[1])
            first = mm(field1(0, y0, n, parity), wm1[0, :, 0:128])
            outs = []
            for f in range(2):
                z = acc[f, parity, y0 * 24 : (y0 + n) * 24, :] + both[:, f * 128 : f * 128 + 128]
                if f == 0:
                    z = z + first
                z = z + b1[...]
                x = p1[2 + f, 1 + y0 : 1 + y0 + n, pl.ds(PAD + parity, 24, stride=2), :]
                outs.append((x.reshape(n * 24, 128) + silu(z)).reshape(n // 2, 2, 24, 128))
            sides.append(outs)
        pieces = []
        for by in range(2):
            for parity in range(2):
                pieces.append(
                    jnp.concatenate(
                        [sides[parity][f][:, by].reshape(n * 12, 128) for f in range(2)], axis=0
                    ).astype(BF16)
                )
        red = (mm(jnp.concatenate(pieces, axis=1), sw[...]) + sb[...]).astype(BF16)
        rsend[b, 0 : n * 24, :] = red

        @pl.when(has_next)
        def _():
            red_copy(b).start()

        wide = red.astype(F32).reshape(2, n // 2, 24, 128)
        for f in range(2):
            p2[2 + f, 1 + y0 // 2 : 1 + y0 // 2 + n // 2, PAD : PAD + 24, :] = wide[f]

    def section_two(b):
        r0, rn = RED[b]

        @pl.when(has_prev)
        def _():
            red_copy(b).wait_recv()

        wide = rrecv[b, 0 : 2 * rn * 24, :].astype(F32).reshape(2, rn, 24, 128)
        for f in range(2):
            p2[f, 1 + r0 : 1 + r0 + rn, PAD : PAD + 24, :] = wide[f]
        y0 = 6 * b
        both = mm(field2(1, y0, 6), wm2[1]) + mm(field2(2, y0, 6), wm2[2])
        ends = (mm(field2(0, y0, 6), wm2[0, :, 0:128]), mm(field2(3, y0, 6), w2[2]))
        for f in range(2):
            z = both[:, f * 128 : f * 128 + 128] + ends[f] + b2[...]
            x = p2[2 + f, 1 + y0 : 7 + y0, PAD : PAD + 24, :].reshape(144, 128)
            fs[f] = x + silu(z)
            for y in range(3):
                for by in range(2):
                    for bx in range(2):
                        lane = (by * 2 + bx) * 128
                        stage[f * 36 + y * 12 : f * 36 + y * 12 + 12, lane : lane + 128] = fs[
                            f, pl.ds(48 * y + 24 * by + bx, 12, stride=2), :
                        ]
        psend[b] = stage[...].astype(BF16)
        patch_own(b).start()
        for k in range(1, n_dp):
            patch_copy(b, k).start()

    for b in range(PIECES):
        section_one(b)
        if b > 0:
            section_two(b - 1)
    section_two(PIECES - 1)

    meta_own().wait()
    for k in range(1, n_dp):
        meta_copy(k).wait()
    for b in range(PIECES):
        patch_own(b).wait()
        for k in range(1, n_dp):
            patch_copy(b, k).wait()

    @pl.when(has_next)
    def _():
        for b in range(PIECES):
            feat_copy(b).wait_send()
            red_copy(b).wait_send()


def embed(n_dp, base, patches, meta, ew, eb, table, out):
    tile = out.shape[0]
    width = meta.shape[2]
    first = pl.program_id(0) * tile
    slot = lax.broadcasted_iota(jnp.int32, (tile, width), 0) + (first + base[0])
    slot = slot.astype(F32)
    bucket_at = lax.broadcasted_iota(jnp.int32, (128, width), 0)
    names = table.shape[0]
    name = lax.rem(bucket_at, names).astype(F32)
    inside = bucket_at < 3 * names
    got = jnp.zeros((tile, patches.shape[2]), F32)
    sel = jnp.zeros((tile, 128), F32)
    for d in range(n_dp):
        hot = jnp.where(slot == meta[d, 0:1, :], 1.0, 0.0).astype(BF16)
        named = jnp.where((name == meta[d, 1:2, :]) & inside, 1.0, 0.0).astype(BF16)
        got = got + jnp.dot(hot, patches[d], preferred_element_type=F32)
        sel = sel + lax.dot_general(
            hot, named, (((1,), (1,)), ((), ())), preferred_element_type=F32
        )
    full = table[...] + eb[...]
    high = full.astype(BF16).astype(F32)
    mid = (full - high).astype(BF16).astype(F32)
    low = full - high - mid
    split = jnp.concatenate(
        [high, mid, low, jnp.zeros((128 - 3 * names, full.shape[1]), F32)], axis=0
    ).astype(BF16)
    total = jnp.dot(got.astype(BF16), ew[...], preferred_element_type=F32)
    total = total + jnp.dot(sel.astype(BF16), split, preferred_element_type=F32)
    out[...] = total.astype(BF16)


def shards(
    n_dp,
    n_tm,
    features,
    frame_counts,
    conv1_weight,
    conv1_bias,
    shrink_weight,
    shrink_bias,
    conv2_weight,
    conv2_bias,
    embed_weight,
    embed_bias,
    bucket_table,
    bucket_ids,
    dest_owner,
    dest_offset,
):
    rows = dest_owner.shape[1]
    pack = 2 * rows
    lat = embed_weight.shape[1]
    block = 80
    wide = PIECES * block
    vmem = pl.BlockSpec(memory_space=pltpu.VMEM)
    anywhere = pl.BlockSpec(memory_space=pl.ANY)
    smem = pl.BlockSpec(memory_space=pltpu.SMEM)
    peers = max(n_dp, 2)
    dma = pltpu.SemaphoreType.DMA
    patches, meta = pl.pallas_call(
        functools.partial(body, rows, pack, n_tm, n_dp, frame_counts.shape[1]),
        out_shape=(
            jax.ShapeDtypeStruct((n_dp, PIECES, block, 512), BF16),
            jax.ShapeDtypeStruct((n_dp, 8, wide), F32),
        ),
        in_specs=[anywhere, smem] + [vmem] * 9,
        out_specs=(anywhere, anywhere),
        scratch_shapes=[
            pltpu.VMEM((2, 48, 48, 128), BF16),
            pltpu.VMEM((2, 48, 48, 128), BF16),
            pltpu.VMEM((4, 50, 48 + 2 * PAD, 128), F32),
            pltpu.VMEM((4, 26, 24 + 2 * PAD, 128), F32),
            pltpu.VMEM((3, 1152, 256), BF16),
            pltpu.VMEM((3, 1152, 256), BF16),
            pltpu.VMEM((2, 2, 48 * 24, 128), F32),
            pltpu.VMEM((PIECES, 336, 128), BF16),
            pltpu.VMEM((PIECES, 336, 128), BF16),
            pltpu.VMEM((2, 144, 128), F32),
            pltpu.VMEM((block, 512), F32),
            pltpu.VMEM((PIECES, block, 512), BF16),
            pltpu.VMEM((8, wide), F32),
            dma,
            dma((PIECES,)),
            dma((PIECES,)),
            dma((PIECES,)),
            dma((PIECES,)),
            dma((PIECES, peers)),
            dma((PIECES, peers)),
            dma((peers,)),
            dma((peers,)),
            dma((PIECES + 1,)),
        ],
        compiler_params=pltpu.CompilerParams(
            collective_id=0, has_side_effects=True, vmem_limit_bytes=56 * 1024 * 1024
        ),
        name="sections",
    )(
        features,
        frame_counts,
        conv1_weight.reshape(3, 1152, 128),
        conv1_bias.reshape(1, 128),
        shrink_weight,
        shrink_bias.reshape(1, 128),
        conv2_weight.reshape(3, 1152, 128),
        conv2_bias.reshape(1, 128),
        bucket_ids,
        dest_owner,
        dest_offset,
    )
    base = (lax.axis_index("dp") * pack + 1).astype(jnp.int32).reshape(1)
    tile = pack // 2
    packed = pl.pallas_call(
        functools.partial(embed, n_dp),
        grid=(pack // tile,),
        out_shape=jax.ShapeDtypeStruct((pack, lat), BF16),
        in_specs=[
            smem,
            pl.BlockSpec((n_dp, wide, 512), lambda i: (0, 0, 0)),
            pl.BlockSpec((n_dp, 8, wide), lambda i: (0, 0, 0)),
            pl.BlockSpec((512, lat), lambda i: (0, 0)),
            pl.BlockSpec((1, lat), lambda i: (0, 0)),
            pl.BlockSpec(bucket_table.shape, lambda i: (0, 0)),
        ],
        out_specs=pl.BlockSpec((tile, lat), lambda i: (i, 0)),
        compiler_params=pltpu.CompilerParams(vmem_limit_bytes=48 * 1024 * 1024),
        name="embed",
    )(
        base,
        patches.reshape(n_dp, wide, 512),
        meta,
        embed_weight,
        embed_bias.reshape(1, lat),
        bucket_table,
    )
    return packed[None]


def solution(mesh):
    sizes = dict(mesh.shape)
    return jax.shard_map(
        functools.partial(shards, sizes["dp"], sizes["tm"]),
        mesh=mesh,
        in_specs=(
            P("dp", "tm", None, None, None),
            P("dp", None),
            P(),
            P(),
            P(),
            P(),
            P(),
            P(),
            P(),
            P(),
            P(),
            P("dp", "tm"),
            P("dp", "tm"),
            P("dp", "tm"),
        ),
        out_specs=P("dp", "tm", None),
        check_vma=False,
    )
```

```python
import functools
import jax
import jax.numpy as jnp
from jax import lax
from jax.experimental import pallas as pl
from jax.experimental.pallas import tpu as pltpu
from jax.sharding import PartitionSpec as P

MESH = pl.DeviceIdType.MESH
F32 = jnp.float32
BF16 = jnp.bfloat16
HALF = 27
FEAT = ((0, 9), (9, 9), (18, 9))
RED = ((0, 3), (3, 5), (8, 5))
PIECES = 3
PAD = 8


def silu(v):
    return v / (1.0 + jnp.exp(-v))


def live_factors(counts_ref, first, videos):
    def segment(moment):
        total = jnp.int32(0)
        bound = jnp.int32(0)
        for i in range(videos):
            bound = bound + counts_ref[0, i]
            total = total + jnp.where(moment >= bound, 1, 0)
        return total

    seg = {d: segment(first + d) for d in (-2, -1, 0, 1)}

    def live(frame, distance):
        same = jnp.where(seg[frame] == seg[frame - distance], 1.0, 0.0)
        there = jnp.where(first + frame - distance >= 0, 1.0, 0.0)
        return (same * there).astype(F32)

    return live


def body(
    rows,
    pack,
    n_tm,
    n_dp,
    videos,
    feat,
    counts,
    w1,
    b1,
    sw,
    sb,
    w2,
    b2,
    bucket,
    owner,
    offset,
    patches_out,
    meta_out,
    raw,
    p1,
    p2,
    wm1,
    wm2,
    rsend,
    rrecv,
    fs,
    stage,
    psend,
    pgot,
    meta,
    local_sem,
    xsend_sem,
    xrecv_sem,
    zsend_sem,
    zrecv_sem,
    rsend_sem,
    rrecv_sem,
    gsend_sem,
    grecv_sem,
    psend_sem,
    precv_sem,
    msend_sem,
    mrecv_sem,
    own_sem,
):
    dp = lax.axis_index("dp")
    tm = lax.axis_index("tm")
    side = lax.rem(tm, 2)
    mate = tm + 1 - 2 * side
    has_next = tm < n_tm - 2
    has_prev = tm > 1
    nxt = lax.rem(tm + 2, n_tm)
    prv = lax.rem(tm + n_tm - 2, n_tm)

    load = pltpu.make_async_copy(
        feat.at[0, :, pl.ds(21 * side, HALF)], raw.at[1 + side], local_sem
    )
    load.start()

    barrier = pltpu.get_barrier_semaphore()
    pl.semaphore_signal(barrier, inc=1, device_id=(dp, mate), device_id_type=MESH)

    @pl.when(has_next)
    def _():
        pl.semaphore_signal(barrier, inc=1, device_id=(dp, nxt), device_id_type=MESH)

    @pl.when(has_prev)
    def _():
        pl.semaphore_signal(barrier, inc=1, device_id=(dp, prv), device_id_type=MESH)

    for k in range(1, n_dp):
        pl.semaphore_signal(
            barrier, inc=1, device_id=(lax.rem(dp + k, n_dp), tm), device_id_type=MESH
        )
    beside = has_next.astype(jnp.int32) + has_prev.astype(jnp.int32)
    pl.semaphore_wait(barrier, n_dp + beside)

    def mate_copy(c):
        y0, n = FEAT[c]
        return pltpu.make_async_remote_copy(
            src_ref=feat.at[0, :, pl.ds(21 * (1 - side) + y0, n)],
            dst_ref=raw.at[1 + side, :, pl.ds(y0, n)],
            send_sem=xsend_sem.at[c],
            recv_sem=xrecv_sem.at[c],
            device_id=(dp, mate),
            device_id_type=MESH,
        )

    def next_copy(c):
        y0, n = FEAT[c]
        return pltpu.make_async_remote_copy(
            src_ref=raw.at[2, :, pl.ds(y0, n)],
            dst_ref=raw.at[0, :, pl.ds(y0, n)],
            send_sem=zsend_sem.at[c],
            recv_sem=zrecv_sem.at[c],
            device_id=(dp, nxt),
            device_id_type=MESH,
        )

    def red_copy(c):
        n = 2 * RED[c][1] * 24
        return pltpu.make_async_remote_copy(
            src_ref=rsend.at[c, pl.ds(0, n)],
            dst_ref=rrecv.at[c, pl.ds(0, n)],
            send_sem=rsend_sem.at[c],
            recv_sem=rrecv_sem.at[c],
            device_id=(dp, nxt),
            device_id_type=MESH,
        )

    def give_copy(e):
        return pltpu.make_async_remote_copy(
            src_ref=psend.at[e],
            dst_ref=pgot,
            send_sem=gsend_sem,
            recv_sem=grecv_sem,
            device_id=(dp, mate),
            device_id_type=MESH,
        )

    def patch_copy(src, half, lot, k):
        return pltpu.make_async_remote_copy(
            src_ref=src,
            dst_ref=patches_out.at[dp, half],
            send_sem=psend_sem.at[lot, k],
            recv_sem=precv_sem.at[lot, k],
            device_id=(lax.rem(dp + k, n_dp), tm),
            device_id_type=MESH,
        )

    def patch_own(src, half, lot):
        return pltpu.make_async_copy(src, patches_out.at[dp, half], own_sem.at[lot])

    def meta_copy(k):
        return pltpu.make_async_remote_copy(
            src_ref=meta,
            dst_ref=meta_out.at[dp],
            send_sem=msend_sem.at[k],
            recv_sem=mrecv_sem.at[k],
            device_id=(lax.rem(dp + k, n_dp), tm),
            device_id_type=MESH,
        )

    def meta_own():
        return pltpu.make_async_copy(meta, meta_out.at[dp], own_sem.at[2])

    for c in range(PIECES):
        mate_copy(c).start()
    load.wait()

    @pl.when(has_next & (side == 1))
    def _():
        for c in range(PIECES):
            next_copy(c).start()

    p1[...] = jnp.zeros(p1.shape, F32)
    p2[...] = jnp.zeros(p2.shape, F32)

    @pl.when(tm <= 1)
    def _():
        rrecv[...] = jnp.zeros(rrecv.shape, BF16)

    frame = rows // 2
    part = frame // 2
    row_at = lax.broadcasted_iota(jnp.int32, (rows, rows), 0)
    col_at = lax.broadcasted_iota(jnp.int32, (rows, rows), 1)
    order = jnp.zeros((rows, rows), F32)
    for b in range(2):
        for f in range(2):
            c0 = b * frame + f * part
            hit = (
                (col_at - row_at == c0 - (f * frame + b * part))
                & (col_at >= c0)
                & (col_at < c0 + part)
            )
            order = order + jnp.where(hit, 1.0, 0.0)
    code = (owner[...] * pack + offset[...] + 1).astype(F32)
    table = jnp.concatenate(
        [code, bucket[...].astype(F32), jnp.zeros((6, rows), F32)], axis=0
    )
    meta[...] = jnp.dot(
        table, order, precision=lax.Precision.HIGHEST, preferred_element_type=F32
    )
    meta_own().start()
    for k in range(1, n_dp):
        meta_copy(k).start()

    for e in range(2):
        live = live_factors(counts, (tm - side) * 2 + 2 * e, videos)
        for w, wm in ((w1, wm1), (w2, wm2)):
            wm[e, 0, :, 0:128] = w[0] * live(0, 2).astype(BF16)
            wm[e, 1, :, 0:128] = w[1] * live(0, 1).astype(BF16)
            wm[e, 1, :, 128:256] = w[0] * live(1, 2).astype(BF16)
            wm[e, 2, :, 0:128] = w[2]
            wm[e, 2, :, 128:256] = w[1] * live(1, 1).astype(BF16)

    def field1(s, y0, n, parity):
        parts = []
        for dy in range(3):
            for dx in range(3):
                v = p1[s, y0 + dy : y0 + dy + n, pl.ds(PAD + parity + dx - 1, 24, stride=2), :]
                parts.append(v.reshape(n * 24, 128).astype(BF16))
        return jnp.concatenate(parts, axis=1)

    def field2(s, n):
        parts = []
        for dy in range(3):
            for dx in range(3):
                v = p2[s, dy : dy + n, PAD + dx - 1 : PAD + dx + 23, :]
                parts.append(v.reshape(n * 24, 128).astype(BF16))
        return jnp.concatenate(parts, axis=1)

    def mm(a, w):
        return jnp.dot(a, w, preferred_element_type=F32)

    def widen(pair, y0, n):
        for f in range(2):
            p1[2 * pair + f, pl.ds(1 - side + y0, n), PAD : PAD + 48, :] = raw[
                pair, f, y0 : y0 + n
            ].astype(F32)

    widen(1 + side, 0, HALF)

    def section_one(e, c):
        f0, fn = FEAT[c]
        if e == 1:
            mate_copy(c).wait_recv()

            @pl.when(has_next & (side == 0))
            def _():
                next_copy(c).start()

            widen(2 - side, f0, fn)
        else:

            @pl.when(has_prev)
            def _():
                next_copy(c).wait_recv()
                widen(0, f0, fn)

        r0, rn = RED[c]
        y0, n = 2 * r0, 2 * rn
        sides = []
        for parity in range(2):
            both = mm(field1(2 * e + 1, y0, n, parity), wm1[e, 1])
            both = both + mm(field1(2 * e + 2, y0, n, parity), wm1[e, 2])
            ends = (
                mm(field1(2 * e, y0, n, parity), wm1[e, 0, :, 0:128]),
                mm(field1(2 * e + 3, y0, n, parity), w1[2]),
            )
            outs = []
            for f in range(2):
                z = both[:, f * 128 : f * 128 + 128] + ends[f] + b1[...]
                x = p1[2 + 2 * e + f, 1 + y0 : 1 + y0 + n, pl.ds(PAD + parity, 24, stride=2), :]
                outs.append((x.reshape(n * 24, 128) + silu(z)).reshape(rn, 2, 24, 128))
            sides.append(outs)
        pieces = []
        for by in range(2):
            for parity in range(2):
                pieces.append(
                    jnp.concatenate(
                        [sides[parity][f][:, by].reshape(rn * 24, 128) for f in range(2)], axis=0
                    ).astype(BF16)
                )
        red = (mm(jnp.concatenate(pieces, axis=1), sw[...]) + sb[...]).astype(BF16)
        if e == 1:
            rsend[c, 0 : 2 * rn * 24, :] = red

            @pl.when(has_next)
            def _():
                red_copy(c).start()

        wide = red.astype(F32).reshape(2, rn, 24, 128)
        for f in range(2):
            p2[2 + 2 * e + f, pl.ds(1 - side + r0, rn), PAD : PAD + 24, :] = wide[f]

    def section_two(e):
        if e == 0:

            @pl.when(has_prev)
            def _():
                for c in range(PIECES):
                    red_copy(c).wait_recv()

            for c in range(PIECES):
                r0, rn = RED[c]
                wide = rrecv[c, 0 : 2 * rn * 24, :].astype(F32).reshape(2, rn, 24, 128)
                for f in range(2):
                    p2[f, pl.ds(1 - side + r0, rn), PAD : PAD + 24, :] = wide[f]
        both = mm(field2(2 * e + 1, 12), wm2[e, 1]) + mm(field2(2 * e + 2, 12), wm2[e, 2])
        ends = (
            mm(field2(2 * e, 12), wm2[e, 0, :, 0:128]),
            mm(field2(2 * e + 3, 12), w2[2]),
        )
        for f in range(2):
            z = both[:, f * 128 : f * 128 + 128] + ends[f] + b2[...]
            x = p2[2 + 2 * e + f, 1:13, PAD : PAD + 24, :].reshape(288, 128)
            fs[f] = x + silu(z)
            for y in range(6):
                for by in range(2):
                    for bx in range(2):
                        lane = (by * 2 + bx) * 128
                        stage[f * 72 + y * 12 : f * 72 + y * 12 + 12, lane : lane + 128] = fs[
                            f, pl.ds(48 * y + 24 * by + bx, 12, stride=2), :
                        ]
        psend[e] = stage[...].astype(BF16)

        @pl.when(side == e)
        def _():
            patch_own(psend.at[e], side, 0).start()
            for k in range(1, n_dp):
                patch_copy(psend.at[e], side, 0, k).start()

        @pl.when(side != e)
        def _():
            give_copy(e).start()

    for e in (1, 0):
        for c in range(PIECES):
            section_one(e, c)
    section_two(1)
    section_two(0)

    give_copy(1 - side).wait_recv()
    patch_own(pgot, 1 - side, 1).start()
    for k in range(1, n_dp):
        patch_copy(pgot, 1 - side, 1, k).start()

    give_copy(1 - side).wait_send()
    meta_own().wait()
    for k in range(1, n_dp):
        meta_copy(k).wait()
    for c in range(PIECES):
        mate_copy(c).wait_send()

    @pl.when(has_next)
    def _():
        for c in range(PIECES):
            next_copy(c).wait_send()
            red_copy(c).wait_send()

    patch_own(psend.at[side], side, 0).wait()
    for k in range(1, n_dp):
        patch_copy(psend.at[side], side, 0, k).wait()
    patch_own(pgot, 1 - side, 1).wait()
    for k in range(1, n_dp):
        patch_copy(pgot, 1 - side, 1, k).wait()


def embed(n_dp, base, patches, meta, ew, eb, table, out):
    tile = out.shape[0]
    width = meta.shape[2]
    first = pl.program_id(0) * tile
    slot = lax.broadcasted_iota(jnp.int32, (tile, width), 0) + (first + base[0])
    slot = slot.astype(F32)
    bucket_at = lax.broadcasted_iota(jnp.int32, (128, width), 0)
    names = table.shape[0]
    name = lax.rem(bucket_at, names).astype(F32)
    inside = bucket_at < 3 * names
    got = jnp.zeros((tile, patches.shape[2]), F32)
    sel = jnp.zeros((tile, 128), F32)
    for d in range(n_dp):
        hot = jnp.where(slot == meta[d, 0:1, :], 1.0, 0.0).astype(BF16)
        named = jnp.where((name == meta[d, 1:2, :]) & inside, 1.0, 0.0).astype(BF16)
        got = got + jnp.dot(hot, patches[d], preferred_element_type=F32)
        sel = sel + lax.dot_general(
            hot, named, (((1,), (1,)), ((), ())), preferred_element_type=F32
        )
    full = table[...] + eb[...]
    high = full.astype(BF16).astype(F32)
    mid = (full - high).astype(BF16).astype(F32)
    low = full - high - mid
    split = jnp.concatenate(
        [high, mid, low, jnp.zeros((128 - 3 * names, full.shape[1]), F32)], axis=0
    ).astype(BF16)
    total = jnp.dot(got.astype(BF16), ew[...], preferred_element_type=F32)
    total = total + jnp.dot(sel.astype(BF16), split, preferred_element_type=F32)
    out[...] = total.astype(BF16)


def shards(
    n_dp,
    n_tm,
    features,
    frame_counts,
    conv1_weight,
    conv1_bias,
    shrink_weight,
    shrink_bias,
    conv2_weight,
    conv2_bias,
    embed_weight,
    embed_bias,
    bucket_table,
    bucket_ids,
    dest_owner,
    dest_offset,
):
    rows = dest_owner.shape[1]
    pack = 2 * rows
    lat = embed_weight.shape[1]
    block = rows // 2
    wide = rows
    vmem = pl.BlockSpec(memory_space=pltpu.VMEM)
    anywhere = pl.BlockSpec(memory_space=pl.ANY)
    smem = pl.BlockSpec(memory_space=pltpu.SMEM)
    peers = max(n_dp, 2)
    dma = pltpu.SemaphoreType.DMA
    patches, meta = pl.pallas_call(
        functools.partial(body, rows, pack, n_tm, n_dp, frame_counts.shape[1]),
        out_shape=(
            jax.ShapeDtypeStruct((n_dp, 2, block, 512), BF16),
            jax.ShapeDtypeStruct((n_dp, 8, wide), F32),
        ),
        in_specs=[anywhere, smem] + [vmem] * 9,
        out_specs=(anywhere, anywhere),
        scratch_shapes=[
            pltpu.VMEM((3, 2, HALF, 48, 128), BF16),
            pltpu.VMEM((6, HALF + 1, 48 + 2 * PAD, 128), F32),
            pltpu.VMEM((6, 14, 24 + 2 * PAD, 128), F32),
            pltpu.VMEM((2, 3, 1152, 256), BF16),
            pltpu.VMEM((2, 3, 1152, 256), BF16),
            pltpu.VMEM((PIECES, 240, 128), BF16),
            pltpu.VMEM((PIECES, 240, 128), BF16),
            pltpu.VMEM((2, 288, 128), F32),
            pltpu.VMEM((block, 512), F32),
            pltpu.VMEM((2, block, 512), BF16),
            pltpu.VMEM((block, 512), BF16),
            pltpu.VMEM((8, wide), F32),
            dma,
            dma((PIECES,)),
            dma((PIECES,)),
            dma((PIECES,)),
            dma((PIECES,)),
            dma((PIECES,)),
            dma((PIECES,)),
            dma,
            dma,
            dma((2, peers)),
            dma((2, peers)),
            dma((peers,)),
            dma((peers,)),
            dma((3,)),
        ],
        compiler_params=pltpu.CompilerParams(
            collective_id=0, has_side_effects=True, vmem_limit_bytes=56 * 1024 * 1024
        ),
        name="sections",
    )(
        features,
        frame_counts,
        conv1_weight.reshape(3, 1152, 128),
        conv1_bias.reshape(1, 128),
        shrink_weight,
        shrink_bias.reshape(1, 128),
        conv2_weight.reshape(3, 1152, 128),
        conv2_bias.reshape(1, 128),
        bucket_ids,
        dest_owner,
        dest_offset,
    )
    base = (lax.axis_index("dp") * pack + 1).astype(jnp.int32).reshape(1)
    tile = pack // 2
    packed = pl.pallas_call(
        functools.partial(embed, n_dp),
        grid=(pack // tile,),
        out_shape=jax.ShapeDtypeStruct((pack, lat), BF16),
        in_specs=[
            smem,
            pl.BlockSpec((n_dp, wide, 512), lambda i: (0, 0, 0)),
            pl.BlockSpec((n_dp, 8, wide), lambda i: (0, 0, 0)),
            pl.BlockSpec((512, lat), lambda i: (0, 0)),
            pl.BlockSpec((1, lat), lambda i: (0, 0)),
            pl.BlockSpec(bucket_table.shape, lambda i: (0, 0)),
        ],
        out_specs=pl.BlockSpec((tile, lat), lambda i: (i, 0)),
        compiler_params=pltpu.CompilerParams(vmem_limit_bytes=48 * 1024 * 1024),
        name="embed",
    )(
        base,
        patches.reshape(n_dp, wide, 512),
        meta,
        embed_weight,
        embed_bias.reshape(1, lat),
        bucket_table,
    )
    return packed[None]


def solution(mesh):
    sizes = dict(mesh.shape)
    return jax.shard_map(
        functools.partial(shards, sizes["dp"], sizes["tm"]),
        mesh=mesh,
        in_specs=(
            P("dp", "tm", None, None, None),
            P("dp", None),
            P(),
            P(),
            P(),
            P(),
            P(),
            P(),
            P(),
            P(),
            P(),
            P("dp", "tm"),
            P("dp", "tm"),
            P("dp", "tm"),
        ),
        out_specs=P("dp", "tm", None),
        check_vma=False,
    )
```

```python
import functools
import jax
import jax.numpy as jnp
from jax import lax
from jax.experimental import pallas as pl
from jax.experimental.pallas import tpu as pltpu
from jax.sharding import PartitionSpec as P

MESH = pl.DeviceIdType.MESH
F32 = jnp.float32
BF16 = jnp.bfloat16
HALF = 27
FEAT = ((0, 9), (9, 9), (18, 9))
RED = ((0, 3), (3, 5), (8, 5))
PIECES = 3
PAD = 8


def silu(v):
    return v / (1.0 + jnp.exp(-v))


def live_factors(counts_ref, first, videos):
    def segment(moment):
        total = jnp.int32(0)
        bound = jnp.int32(0)
        for i in range(videos):
            bound = bound + counts_ref[0, i]
            total = total + jnp.where(moment >= bound, 1, 0)
        return total

    seg = {d: segment(first + d) for d in (-2, -1, 0, 1)}

    def live(frame, distance):
        same = jnp.where(seg[frame] == seg[frame - distance], 1.0, 0.0)
        there = jnp.where(first + frame - distance >= 0, 1.0, 0.0)
        return (same * there).astype(F32)

    return live


def body(
    rows,
    pack,
    n_tm,
    n_dp,
    videos,
    feat,
    counts,
    w1,
    b1,
    sw,
    sb,
    w2,
    b2,
    bucket,
    owner,
    offset,
    patches_out,
    meta_out,
    raw,
    p1,
    p2,
    wm1,
    wm2,
    rsend,
    rrecv,
    fs,
    stage,
    psend,
    pgot,
    meta,
    local_sem,
    xsend_sem,
    xrecv_sem,
    zsend_sem,
    zrecv_sem,
    rsend_sem,
    rrecv_sem,
    gsend_sem,
    grecv_sem,
    psend_sem,
    precv_sem,
    msend_sem,
    mrecv_sem,
    own_sem,
):
    dp = lax.axis_index("dp")
    tm = lax.axis_index("tm")
    side = lax.rem(tm, 2)
    mate = tm + 1 - 2 * side
    has_next = tm < n_tm - 2
    has_prev = tm > 1
    nxt = lax.rem(tm + 2, n_tm)
    prv = lax.rem(tm + n_tm - 2, n_tm)

    load = pltpu.make_async_copy(
        feat.at[0, :, pl.ds(21 * side, HALF)], raw.at[1 + side], local_sem
    )
    load.start()

    barrier = pltpu.get_barrier_semaphore()
    pl.semaphore_signal(barrier, inc=1, device_id=(dp, mate), device_id_type=MESH)

    @pl.when(has_next)
    def _():
        pl.semaphore_signal(barrier, inc=1, device_id=(dp, nxt), device_id_type=MESH)

    @pl.when(has_prev)
    def _():
        pl.semaphore_signal(barrier, inc=1, device_id=(dp, prv), device_id_type=MESH)

    for k in range(1, n_dp):
        pl.semaphore_signal(
            barrier, inc=1, device_id=(lax.rem(dp + k, n_dp), tm), device_id_type=MESH
        )
    beside = has_next.astype(jnp.int32) + has_prev.astype(jnp.int32)
    pl.semaphore_wait(barrier, n_dp + beside)

    def mate_copy(c):
        y0, n = FEAT[c]
        return pltpu.make_async_remote_copy(
            src_ref=feat.at[0, :, pl.ds(21 * (1 - side) + y0, n)],
            dst_ref=raw.at[1 + side, :, pl.ds(y0, n)],
            send_sem=xsend_sem.at[c],
            recv_sem=xrecv_sem.at[c],
            device_id=(dp, mate),
            device_id_type=MESH,
        )

    def next_copy(c):
        y0, n = FEAT[c]
        return pltpu.make_async_remote_copy(
            src_ref=raw.at[2, :, pl.ds(y0, n)],
            dst_ref=raw.at[0, :, pl.ds(y0, n)],
            send_sem=zsend_sem.at[c],
            recv_sem=zrecv_sem.at[c],
            device_id=(dp, nxt),
            device_id_type=MESH,
        )

    def red_copy(c):
        n = 2 * RED[c][1] * 24
        return pltpu.make_async_remote_copy(
            src_ref=rsend.at[c, pl.ds(0, n)],
            dst_ref=rrecv.at[c, pl.ds(0, n)],
            send_sem=rsend_sem.at[c],
            recv_sem=rrecv_sem.at[c],
            device_id=(dp, nxt),
            device_id_type=MESH,
        )

    def give_copy(e):
        return pltpu.make_async_remote_copy(
            src_ref=psend.at[e],
            dst_ref=pgot,
            send_sem=gsend_sem,
            recv_sem=grecv_sem,
            device_id=(dp, mate),
            device_id_type=MESH,
        )

    def patch_copy(src, half, lot, k):
        return pltpu.make_async_remote_copy(
            src_ref=src,
            dst_ref=patches_out.at[dp, half],
            send_sem=psend_sem.at[lot, k],
            recv_sem=precv_sem.at[lot, k],
            device_id=(lax.rem(dp + k, n_dp), tm),
            device_id_type=MESH,
        )

    def patch_own(src, half, lot):
        return pltpu.make_async_copy(src, patches_out.at[dp, half], own_sem.at[lot])

    def meta_copy(k):
        return pltpu.make_async_remote_copy(
            src_ref=meta,
            dst_ref=meta_out.at[dp],
            send_sem=msend_sem.at[k],
            recv_sem=mrecv_sem.at[k],
            device_id=(lax.rem(dp + k, n_dp), tm),
            device_id_type=MESH,
        )

    def meta_own():
        return pltpu.make_async_copy(meta, meta_out.at[dp], own_sem.at[2])

    mate_copy(0).start()
    load.wait()

    @pl.when(has_next & (side == 1))
    def _():
        for c in range(PIECES):
            next_copy(c).start()

    p1[...] = jnp.zeros(p1.shape, F32)
    p2[...] = jnp.zeros(p2.shape, F32)

    @pl.when(tm <= 1)
    def _():
        rrecv[...] = jnp.zeros(rrecv.shape, BF16)

    frame = rows // 2
    part = frame // 2
    row_at = lax.broadcasted_iota(jnp.int32, (rows, rows), 0)
    col_at = lax.broadcasted_iota(jnp.int32, (rows, rows), 1)
    order = jnp.zeros((rows, rows), F32)
    for b in range(2):
        for f in range(2):
            c0 = b * frame + f * part
            hit = (
                (col_at - row_at == c0 - (f * frame + b * part))
                & (col_at >= c0)
                & (col_at < c0 + part)
            )
            order = order + jnp.where(hit, 1.0, 0.0)
    code = (owner[...] * pack + offset[...] + 1).astype(F32)
    table = jnp.concatenate(
        [code, bucket[...].astype(F32), jnp.zeros((6, rows), F32)], axis=0
    )
    meta[...] = jnp.dot(
        table, order, precision=lax.Precision.HIGHEST, preferred_element_type=F32
    )
    meta_own().start()
    for k in range(1, n_dp):
        meta_copy(k).start()

    for e in range(2):
        live = live_factors(counts, (tm - side) * 2 + 2 * e, videos)
        for w, wm in ((w1, wm1), (w2, wm2)):
            wm[e, 0, :, 0:128] = w[0] * live(0, 2).astype(BF16)
            wm[e, 1, :, 0:128] = w[1] * live(0, 1).astype(BF16)
            wm[e, 1, :, 128:256] = w[0] * live(1, 2).astype(BF16)
            wm[e, 2, :, 0:128] = w[2]
            wm[e, 2, :, 128:256] = w[1] * live(1, 1).astype(BF16)

    def field1(s, y0, n, parity):
        parts = []
        for dy in range(3):
            for dx in range(3):
                v = p1[s, y0 + dy : y0 + dy + n, pl.ds(PAD + parity + dx - 1, 24, stride=2), :]
                parts.append(v.reshape(n * 24, 128).astype(BF16))
        return jnp.concatenate(parts, axis=1)

    def field2(s, n):
        parts = []
        for dy in range(3):
            for dx in range(3):
                v = p2[s, dy : dy + n, PAD + dx - 1 : PAD + dx + 23, :]
                parts.append(v.reshape(n * 24, 128).astype(BF16))
        return jnp.concatenate(parts, axis=1)

    def mm(a, w):
        return jnp.dot(a, w, preferred_element_type=F32)

    def widen(pair, y0, n):
        for f in range(2):
            p1[2 * pair + f, pl.ds(1 - side + y0, n), PAD : PAD + 48, :] = raw[
                pair, f, y0 : y0 + n
            ].astype(F32)

    widen(1 + side, 0, HALF)

    def section_one(e, c):
        f0, fn = FEAT[c]
        if e == 1:
            mate_copy(c).wait_send()
            if c + 1 < PIECES:
                mate_copy(c + 1).start()
            mate_copy(c).wait_recv()

            @pl.when(has_next & (side == 0))
            def _():
                next_copy(c).start()

            widen(2 - side, f0, fn)
        else:

            @pl.when(has_prev)
            def _():
                next_copy(c).wait_recv()
                widen(0, f0, fn)

        r0, rn = RED[c]
        y0, n = 2 * r0, 2 * rn
        sides = []
        for parity in range(2):
            both = mm(field1(2 * e + 1, y0, n, parity), wm1[e, 1])
            both = both + mm(field1(2 * e + 2, y0, n, parity), wm1[e, 2])
            ends = (
                mm(field1(2 * e, y0, n, parity), wm1[e, 0, :, 0:128]),
                mm(field1(2 * e + 3, y0, n, parity), w1[2]),
            )
            outs = []
            for f in range(2):
                z = both[:, f * 128 : f * 128 + 128] + ends[f] + b1[...]
                x = p1[2 + 2 * e + f, 1 + y0 : 1 + y0 + n, pl.ds(PAD + parity, 24, stride=2), :]
                outs.append((x.reshape(n * 24, 128) + silu(z)).reshape(rn, 2, 24, 128))
            sides.append(outs)
        pieces = []
        for by in range(2):
            for parity in range(2):
                pieces.append(
                    jnp.concatenate(
                        [sides[parity][f][:, by].reshape(rn * 24, 128) for f in range(2)], axis=0
                    ).astype(BF16)
                )
        red = (mm(jnp.concatenate(pieces, axis=1), sw[...]) + sb[...]).astype(BF16)
        if e == 1:
            rsend[c, 0 : 2 * rn * 24, :] = red

            @pl.when(has_next)
            def _():
                red_copy(c).start()

        wide = red.astype(F32).reshape(2, rn, 24, 128)
        for f in range(2):
            p2[2 + 2 * e + f, pl.ds(1 - side + r0, rn), PAD : PAD + 24, :] = wide[f]

    def section_two(e):
        if e == 0:

            @pl.when(has_prev)
            def _():
                for c in range(PIECES):
                    red_copy(c).wait_recv()

            for c in range(PIECES):
                r0, rn = RED[c]
                wide = rrecv[c, 0 : 2 * rn * 24, :].astype(F32).reshape(2, rn, 24, 128)
                for f in range(2):
                    p2[f, pl.ds(1 - side + r0, rn), PAD : PAD + 24, :] = wide[f]
        both = mm(field2(2 * e + 1, 12), wm2[e, 1]) + mm(field2(2 * e + 2, 12), wm2[e, 2])
        ends = (
            mm(field2(2 * e, 12), wm2[e, 0, :, 0:128]),
            mm(field2(2 * e + 3, 12), w2[2]),
        )
        for f in range(2):
            z = both[:, f * 128 : f * 128 + 128] + ends[f] + b2[...]
            x = p2[2 + 2 * e + f, 1:13, PAD : PAD + 24, :].reshape(288, 128)
            fs[f] = x + silu(z)
            for y in range(6):
                for by in range(2):
                    for bx in range(2):
                        lane = (by * 2 + bx) * 128
                        stage[f * 72 + y * 12 : f * 72 + y * 12 + 12, lane : lane + 128] = fs[
                            f, pl.ds(48 * y + 24 * by + bx, 12, stride=2), :
                        ]
        psend[e] = stage[...].astype(BF16)

        @pl.when(side == e)
        def _():
            patch_own(psend.at[e], side, 0).start()
            for k in range(1, n_dp):
                patch_copy(psend.at[e], side, 0, k).start()

        @pl.when(side != e)
        def _():
            give_copy(e).start()

    for e in (1, 0):
        for c in range(PIECES):
            section_one(e, c)
    section_two(1)
    section_two(0)

    give_copy(1 - side).wait_recv()
    patch_own(pgot, 1 - side, 1).start()
    for k in range(1, n_dp):
        patch_copy(pgot, 1 - side, 1, k).start()

    give_copy(1 - side).wait_send()
    meta_own().wait()
    for k in range(1, n_dp):
        meta_copy(k).wait()
    @pl.when(has_next)
    def _():
        for c in range(PIECES):
            next_copy(c).wait_send()
            red_copy(c).wait_send()

    patch_own(psend.at[side], side, 0).wait()
    for k in range(1, n_dp):
        patch_copy(psend.at[side], side, 0, k).wait()
    patch_own(pgot, 1 - side, 1).wait()
    for k in range(1, n_dp):
        patch_copy(pgot, 1 - side, 1, k).wait()


def embed(n_dp, base, patches, meta, ew, eb, table, out):
    tile = out.shape[0]
    width = meta.shape[2]
    first = pl.program_id(0) * tile
    slot = lax.broadcasted_iota(jnp.int32, (tile, width), 0) + (first + base[0])
    slot = slot.astype(F32)
    bucket_at = lax.broadcasted_iota(jnp.int32, (128, width), 0)
    names = table.shape[0]
    name = lax.rem(bucket_at, names).astype(F32)
    inside = bucket_at < 3 * names
    got = jnp.zeros((tile, patches.shape[2]), F32)
    sel = jnp.zeros((tile, 128), F32)
    for d in range(n_dp):
        hot = jnp.where(slot == meta[d, 0:1, :], 1.0, 0.0).astype(BF16)
        named = jnp.where((name == meta[d, 1:2, :]) & inside, 1.0, 0.0).astype(BF16)
        got = got + jnp.dot(hot, patches[d], preferred_element_type=F32)
        sel = sel + lax.dot_general(
            hot, named, (((1,), (1,)), ((), ())), preferred_element_type=F32
        )
    full = table[...] + eb[...]
    high = full.astype(BF16).astype(F32)
    mid = (full - high).astype(BF16).astype(F32)
    low = full - high - mid
    split = jnp.concatenate(
        [high, mid, low, jnp.zeros((128 - 3 * names, full.shape[1]), F32)], axis=0
    ).astype(BF16)
    total = jnp.dot(got.astype(BF16), ew[...], preferred_element_type=F32)
    total = total + jnp.dot(sel.astype(BF16), split, preferred_element_type=F32)
    out[...] = total.astype(BF16)


def shards(
    n_dp,
    n_tm,
    features,
    frame_counts,
    conv1_weight,
    conv1_bias,
    shrink_weight,
    shrink_bias,
    conv2_weight,
    conv2_bias,
    embed_weight,
    embed_bias,
    bucket_table,
    bucket_ids,
    dest_owner,
    dest_offset,
):
    rows = dest_owner.shape[1]
    pack = 2 * rows
    lat = embed_weight.shape[1]
    block = rows // 2
    wide = rows
    vmem = pl.BlockSpec(memory_space=pltpu.VMEM)
    anywhere = pl.BlockSpec(memory_space=pl.ANY)
    smem = pl.BlockSpec(memory_space=pltpu.SMEM)
    peers = max(n_dp, 2)
    dma = pltpu.SemaphoreType.DMA
    patches, meta = pl.pallas_call(
        functools.partial(body, rows, pack, n_tm, n_dp, frame_counts.shape[1]),
        out_shape=(
            jax.ShapeDtypeStruct((n_dp, 2, block, 512), BF16),
            jax.ShapeDtypeStruct((n_dp, 8, wide), F32),
        ),
        in_specs=[anywhere, smem] + [vmem] * 9,
        out_specs=(anywhere, anywhere),
        scratch_shapes=[
            pltpu.VMEM((3, 2, HALF, 48, 128), BF16),
            pltpu.VMEM((6, HALF + 1, 48 + 2 * PAD, 128), F32),
            pltpu.VMEM((6, 14, 24 + 2 * PAD, 128), F32),
            pltpu.VMEM((2, 3, 1152, 256), BF16),
            pltpu.VMEM((2, 3, 1152, 256), BF16),
            pltpu.VMEM((PIECES, 240, 128), BF16),
            pltpu.VMEM((PIECES, 240, 128), BF16),
            pltpu.VMEM((2, 288, 128), F32),
            pltpu.VMEM((block, 512), F32),
            pltpu.VMEM((2, block, 512), BF16),
            pltpu.VMEM((block, 512), BF16),
            pltpu.VMEM((8, wide), F32),
            dma,
            dma((PIECES,)),
            dma((PIECES,)),
            dma((PIECES,)),
            dma((PIECES,)),
            dma((PIECES,)),
            dma((PIECES,)),
            dma,
            dma,
            dma((2, peers)),
            dma((2, peers)),
            dma((peers,)),
            dma((peers,)),
            dma((3,)),
        ],
        compiler_params=pltpu.CompilerParams(
            collective_id=0, has_side_effects=True, vmem_limit_bytes=56 * 1024 * 1024
        ),
        name="sections",
    )(
        features,
        frame_counts,
        conv1_weight.reshape(3, 1152, 128),
        conv1_bias.reshape(1, 128),
        shrink_weight,
        shrink_bias.reshape(1, 128),
        conv2_weight.reshape(3, 1152, 128),
        conv2_bias.reshape(1, 128),
        bucket_ids,
        dest_owner,
        dest_offset,
    )
    base = (lax.axis_index("dp") * pack + 1).astype(jnp.int32).reshape(1)
    tile = pack // 2
    packed = pl.pallas_call(
        functools.partial(embed, n_dp),
        grid=(pack // tile,),
        out_shape=jax.ShapeDtypeStruct((pack, lat), BF16),
        in_specs=[
            smem,
            pl.BlockSpec((n_dp, wide, 512), lambda i: (0, 0, 0)),
            pl.BlockSpec((n_dp, 8, wide), lambda i: (0, 0, 0)),
            pl.BlockSpec((512, lat), lambda i: (0, 0)),
            pl.BlockSpec((1, lat), lambda i: (0, 0)),
            pl.BlockSpec(bucket_table.shape, lambda i: (0, 0)),
        ],
        out_specs=pl.BlockSpec((tile, lat), lambda i: (i, 0)),
        compiler_params=pltpu.CompilerParams(vmem_limit_bytes=48 * 1024 * 1024),
        name="embed",
    )(
        base,
        patches.reshape(n_dp, wide, 512),
        meta,
        embed_weight,
        embed_bias.reshape(1, lat),
        bucket_table,
    )
    return packed[None]


def solution(mesh):
    sizes = dict(mesh.shape)
    return jax.shard_map(
        functools.partial(shards, sizes["dp"], sizes["tm"]),
        mesh=mesh,
        in_specs=(
            P("dp", "tm", None, None, None),
            P("dp", None),
            P(),
            P(),
            P(),
            P(),
            P(),
            P(),
            P(),
            P(),
            P(),
            P("dp", "tm"),
            P("dp", "tm"),
            P("dp", "tm"),
        ),
        out_specs=P("dp", "tm", None),
        check_vma=False,
    )
```

```python
import functools
import jax
import jax.numpy as jnp
from jax import lax
from jax.experimental import pallas as pl
from jax.experimental.pallas import tpu as pltpu
from jax.sharding import PartitionSpec as P

MESH = pl.DeviceIdType.MESH
F32 = jnp.float32
BF16 = jnp.bfloat16
HALF = 27
FEAT = ((0, 9), (9, 9), (18, 9))
RED = ((0, 3), (3, 5), (8, 5))
PIECES = 3
PAD = 8


def silu(v):
    return v / (1.0 + jnp.exp(-v))


def live_factors(counts_ref, first, videos):
    def segment(moment):
        total = jnp.int32(0)
        bound = jnp.int32(0)
        for i in range(videos):
            bound = bound + counts_ref[0, i]
            total = total + jnp.where(moment >= bound, 1, 0)
        return total

    seg = {d: segment(first + d) for d in (-2, -1, 0, 1)}

    def live(frame, distance):
        same = jnp.where(seg[frame] == seg[frame - distance], 1.0, 0.0)
        there = jnp.where(first + frame - distance >= 0, 1.0, 0.0)
        return (same * there).astype(F32)

    return live


def body(
    rows,
    pack,
    n_tm,
    n_dp,
    videos,
    feat,
    counts,
    w1,
    b1,
    sw,
    sb,
    w2,
    b2,
    bucket,
    owner,
    offset,
    patches_out,
    meta_out,
    raw,
    p1,
    p2,
    wm1,
    wm2,
    rsend,
    rrecv,
    fs,
    stage,
    psend,
    pgot,
    meta,
    local_sem,
    xsend_sem,
    xrecv_sem,
    zsend_sem,
    zrecv_sem,
    rsend_sem,
    rrecv_sem,
    gsend_sem,
    grecv_sem,
    psend_sem,
    precv_sem,
    msend_sem,
    mrecv_sem,
    own_sem,
):
    dp = lax.axis_index("dp")
    tm = lax.axis_index("tm")
    side = lax.rem(tm, 2)
    mate = tm + 1 - 2 * side
    has_next = tm < n_tm - 2
    has_prev = tm > 1
    nxt = lax.rem(tm + 2, n_tm)
    prv = lax.rem(tm + n_tm - 2, n_tm)
    twin = dp + 1 - 2 * lax.rem(dp, 2)
    pairs = n_dp // 2

    load = pltpu.make_async_copy(
        feat.at[0, :, pl.ds(21 * side, HALF)], raw.at[1 + side], local_sem
    )
    load.start()

    barrier = pltpu.get_barrier_semaphore()
    pl.semaphore_signal(barrier, inc=1, device_id=(dp, mate), device_id_type=MESH)

    @pl.when(has_next)
    def _():
        pl.semaphore_signal(barrier, inc=1, device_id=(dp, nxt), device_id_type=MESH)

    @pl.when(has_prev)
    def _():
        pl.semaphore_signal(barrier, inc=1, device_id=(dp, prv), device_id_type=MESH)

    for k in range(1, n_dp):
        pl.semaphore_signal(
            barrier, inc=1, device_id=(lax.rem(dp + k, n_dp), tm), device_id_type=MESH
        )
    beside = has_next.astype(jnp.int32) + has_prev.astype(jnp.int32)
    pl.semaphore_wait(barrier, n_dp + beside)

    def mate_copy(c):
        y0, n = FEAT[c]
        return pltpu.make_async_remote_copy(
            src_ref=feat.at[0, :, pl.ds(21 * (1 - side) + y0, n)],
            dst_ref=raw.at[1 + side, :, pl.ds(y0, n)],
            send_sem=xsend_sem.at[c],
            recv_sem=xrecv_sem.at[c],
            device_id=(dp, mate),
            device_id_type=MESH,
        )

    def next_copy(c):
        y0, n = FEAT[c]
        return pltpu.make_async_remote_copy(
            src_ref=raw.at[2, :, pl.ds(y0, n)],
            dst_ref=raw.at[0, :, pl.ds(y0, n)],
            send_sem=zsend_sem.at[c],
            recv_sem=zrecv_sem.at[c],
            device_id=(dp, nxt),
            device_id_type=MESH,
        )

    def red_copy(c):
        n = 2 * RED[c][1] * 24
        return pltpu.make_async_remote_copy(
            src_ref=rsend.at[c, pl.ds(0, n)],
            dst_ref=rrecv.at[c, pl.ds(0, n)],
            send_sem=rsend_sem.at[c],
            recv_sem=rrecv_sem.at[c],
            device_id=(dp, nxt),
            device_id_type=MESH,
        )

    def give_copy(e):
        return pltpu.make_async_remote_copy(
            src_ref=psend.at[e],
            dst_ref=pgot,
            send_sem=gsend_sem,
            recv_sem=grecv_sem,
            device_id=(dp, mate),
            device_id_type=MESH,
        )

    def patch_copy(src, half, lot, k):
        return pltpu.make_async_remote_copy(
            src_ref=src,
            dst_ref=patches_out.at[dp, half],
            send_sem=psend_sem.at[lot, k],
            recv_sem=precv_sem.at[lot, k],
            device_id=(lax.rem(dp + 2 * k, n_dp) if k else twin, tm),
            device_id_type=MESH,
        )

    def pass_copy(half, lot, k):
        origin = lax.rem(dp + n_dp - 2 * k, n_dp)
        return pltpu.make_async_remote_copy(
            src_ref=patches_out.at[origin, half],
            dst_ref=patches_out.at[origin, half],
            send_sem=psend_sem.at[lot, pairs + k],
            recv_sem=precv_sem.at[lot, pairs + k],
            device_id=(twin, tm),
            device_id_type=MESH,
        )

    def patch_own(src, half, lot):
        return pltpu.make_async_copy(src, patches_out.at[dp, half], own_sem.at[lot])

    def meta_copy(k):
        return pltpu.make_async_remote_copy(
            src_ref=meta,
            dst_ref=meta_out.at[dp],
            send_sem=msend_sem.at[k],
            recv_sem=mrecv_sem.at[k],
            device_id=(lax.rem(dp + k, n_dp), tm),
            device_id_type=MESH,
        )

    def meta_own():
        return pltpu.make_async_copy(meta, meta_out.at[dp], own_sem.at[2])

    mate_copy(0).start()
    load.wait()

    @pl.when(has_next & (side == 1))
    def _():
        for c in range(PIECES):
            next_copy(c).start()

    p1[...] = jnp.zeros(p1.shape, F32)
    p2[...] = jnp.zeros(p2.shape, F32)

    @pl.when(tm <= 1)
    def _():
        rrecv[...] = jnp.zeros(rrecv.shape, BF16)

    frame = rows // 2
    part = frame // 2
    row_at = lax.broadcasted_iota(jnp.int32, (rows, rows), 0)
    col_at = lax.broadcasted_iota(jnp.int32, (rows, rows), 1)
    order = jnp.zeros((rows, rows), F32)
    for b in range(2):
        for f in range(2):
            c0 = b * frame + f * part
            hit = (
                (col_at - row_at == c0 - (f * frame + b * part))
                & (col_at >= c0)
                & (col_at < c0 + part)
            )
            order = order + jnp.where(hit, 1.0, 0.0)
    code = (owner[...] * pack + offset[...] + 1).astype(F32)
    table = jnp.concatenate(
        [code, bucket[...].astype(F32), jnp.zeros((6, rows), F32)], axis=0
    )
    meta[...] = jnp.dot(
        table, order, precision=lax.Precision.HIGHEST, preferred_element_type=F32
    )
    meta_own().start()
    for k in range(1, n_dp):
        meta_copy(k).start()

    for e in range(2):
        live = live_factors(counts, (tm - side) * 2 + 2 * e, videos)
        for w, wm in ((w1, wm1), (w2, wm2)):
            wm[e, 0, :, 0:128] = w[0] * live(0, 2).astype(BF16)
            wm[e, 1, :, 0:128] = w[1] * live(0, 1).astype(BF16)
            wm[e, 1, :, 128:256] = w[0] * live(1, 2).astype(BF16)
            wm[e, 2, :, 0:128] = w[2]
            wm[e, 2, :, 128:256] = w[1] * live(1, 1).astype(BF16)

    def field1(s, y0, n, parity):
        parts = []
        for dy in range(3):
            for dx in range(3):
                v = p1[s, y0 + dy : y0 + dy + n, pl.ds(PAD + parity + dx - 1, 24, stride=2), :]
                parts.append(v.reshape(n * 24, 128).astype(BF16))
        return jnp.concatenate(parts, axis=1)

    def field2(s, n):
        parts = []
        for dy in range(3):
            for dx in range(3):
                v = p2[s, dy : dy + n, PAD + dx - 1 : PAD + dx + 23, :]
                parts.append(v.reshape(n * 24, 128).astype(BF16))
        return jnp.concatenate(parts, axis=1)

    def mm(a, w):
        return jnp.dot(a, w, preferred_element_type=F32)

    def widen(pair, y0, n):
        for f in range(2):
            p1[2 * pair + f, pl.ds(1 - side + y0, n), PAD : PAD + 48, :] = raw[
                pair, f, y0 : y0 + n
            ].astype(F32)

    widen(1 + side, 0, HALF)

    def section_one(e, c):
        f0, fn = FEAT[c]
        if e == 1:
            mate_copy(c).wait_send()
            if c + 1 < PIECES:
                mate_copy(c + 1).start()
            mate_copy(c).wait_recv()

            @pl.when(has_next & (side == 0))
            def _():
                next_copy(c).start()

            widen(2 - side, f0, fn)
        else:

            @pl.when(has_prev)
            def _():
                next_copy(c).wait_recv()
                widen(0, f0, fn)

        r0, rn = RED[c]
        y0, n = 2 * r0, 2 * rn
        sides = []
        for parity in range(2):
            both = mm(field1(2 * e + 1, y0, n, parity), wm1[e, 1])
            both = both + mm(field1(2 * e + 2, y0, n, parity), wm1[e, 2])
            ends = (
                mm(field1(2 * e, y0, n, parity), wm1[e, 0, :, 0:128]),
                mm(field1(2 * e + 3, y0, n, parity), w1[2]),
            )
            outs = []
            for f in range(2):
                z = both[:, f * 128 : f * 128 + 128] + ends[f] + b1[...]
                x = p1[2 + 2 * e + f, 1 + y0 : 1 + y0 + n, pl.ds(PAD + parity, 24, stride=2), :]
                outs.append((x.reshape(n * 24, 128) + silu(z)).reshape(rn, 2, 24, 128))
            sides.append(outs)
        pieces = []
        for by in range(2):
            for parity in range(2):
                pieces.append(
                    jnp.concatenate(
                        [sides[parity][f][:, by].reshape(rn * 24, 128) for f in range(2)], axis=0
                    ).astype(BF16)
                )
        red = (mm(jnp.concatenate(pieces, axis=1), sw[...]) + sb[...]).astype(BF16)
        if e == 1:
            rsend[c, 0 : 2 * rn * 24, :] = red

            @pl.when(has_next)
            def _():
                red_copy(c).start()

        wide = red.astype(F32).reshape(2, rn, 24, 128)
        for f in range(2):
            p2[2 + 2 * e + f, pl.ds(1 - side + r0, rn), PAD : PAD + 24, :] = wide[f]

    def section_two(e):
        if e == 0:

            @pl.when(has_prev)
            def _():
                for c in range(PIECES):
                    red_copy(c).wait_recv()

            for c in range(PIECES):
                r0, rn = RED[c]
                wide = rrecv[c, 0 : 2 * rn * 24, :].astype(F32).reshape(2, rn, 24, 128)
                for f in range(2):
                    p2[f, pl.ds(1 - side + r0, rn), PAD : PAD + 24, :] = wide[f]
        both = mm(field2(2 * e + 1, 12), wm2[e, 1]) + mm(field2(2 * e + 2, 12), wm2[e, 2])
        ends = (
            mm(field2(2 * e, 12), wm2[e, 0, :, 0:128]),
            mm(field2(2 * e + 3, 12), w2[2]),
        )
        for f in range(2):
            z = both[:, f * 128 : f * 128 + 128] + ends[f] + b2[...]
            x = p2[2 + 2 * e + f, 1:13, PAD : PAD + 24, :].reshape(288, 128)
            fs[f] = x + silu(z)
            for y in range(6):
                for by in range(2):
                    for bx in range(2):
                        lane = (by * 2 + bx) * 128
                        stage[f * 72 + y * 12 : f * 72 + y * 12 + 12, lane : lane + 128] = fs[
                            f, pl.ds(48 * y + 24 * by + bx, 12, stride=2), :
                        ]
        psend[e] = stage[...].astype(BF16)

        @pl.when(side == e)
        def _():
            patch_own(psend.at[e], side, 0).start()
            for k in range(pairs):
                patch_copy(psend.at[e], side, 0, k).start()

        @pl.when(side != e)
        def _():
            give_copy(e).start()

    for e in (1, 0):
        for c in range(PIECES):
            section_one(e, c)
    section_two(1)
    section_two(0)

    give_copy(1 - side).wait_recv()
    patch_own(pgot, 1 - side, 1).start()
    for k in range(pairs):
        patch_copy(pgot, 1 - side, 1, k).start()
    lots = ((psend.at[side], side), (pgot, 1 - side))
    for lot in range(2):
        for k in range(1, pairs):
            patch_copy(lots[lot][0], lots[lot][1], lot, k).wait_recv()
            pass_copy(lots[lot][1], lot, k).start()

    give_copy(1 - side).wait_send()
    meta_own().wait()
    for k in range(1, n_dp):
        meta_copy(k).wait()
    @pl.when(has_next)
    def _():
        for c in range(PIECES):
            next_copy(c).wait_send()
            red_copy(c).wait_send()

    for lot in range(2):
        src, half = lots[lot]
        patch_own(src, half, lot).wait()
        patch_copy(src, half, lot, 0).wait()
        for k in range(1, pairs):
            patch_copy(src, half, lot, k).wait_send()
            pass_copy(half, lot, k).wait()


def embed(n_dp, base, patches, meta, ew, eb, table, out):
    tile = out.shape[0]
    width = meta.shape[2]
    first = pl.program_id(0) * tile
    slot = lax.broadcasted_iota(jnp.int32, (tile, width), 0) + (first + base[0])
    slot = slot.astype(F32)
    bucket_at = lax.broadcasted_iota(jnp.int32, (128, width), 0)
    names = table.shape[0]
    name = lax.rem(bucket_at, names).astype(F32)
    inside = bucket_at < 3 * names
    got = jnp.zeros((tile, patches.shape[2]), F32)
    sel = jnp.zeros((tile, 128), F32)
    for d in range(n_dp):
        hot = jnp.where(slot == meta[d, 0:1, :], 1.0, 0.0).astype(BF16)
        named = jnp.where((name == meta[d, 1:2, :]) & inside, 1.0, 0.0).astype(BF16)
        got = got + jnp.dot(hot, patches[d], preferred_element_type=F32)
        sel = sel + lax.dot_general(
            hot, named, (((1,), (1,)), ((), ())), preferred_element_type=F32
        )
    full = table[...] + eb[...]
    high = full.astype(BF16).astype(F32)
    mid = (full - high).astype(BF16).astype(F32)
    low = full - high - mid
    split = jnp.concatenate(
        [high, mid, low, jnp.zeros((128 - 3 * names, full.shape[1]), F32)], axis=0
    ).astype(BF16)
    total = jnp.dot(got.astype(BF16), ew[...], preferred_element_type=F32)
    total = total + jnp.dot(sel.astype(BF16), split, preferred_element_type=F32)
    out[...] = total.astype(BF16)


def shards(
    n_dp,
    n_tm,
    features,
    frame_counts,
    conv1_weight,
    conv1_bias,
    shrink_weight,
    shrink_bias,
    conv2_weight,
    conv2_bias,
    embed_weight,
    embed_bias,
    bucket_table,
    bucket_ids,
    dest_owner,
    dest_offset,
):
    rows = dest_owner.shape[1]
    pack = 2 * rows
    lat = embed_weight.shape[1]
    block = rows // 2
    wide = rows
    vmem = pl.BlockSpec(memory_space=pltpu.VMEM)
    anywhere = pl.BlockSpec(memory_space=pl.ANY)
    smem = pl.BlockSpec(memory_space=pltpu.SMEM)
    peers = max(n_dp, 2)
    dma = pltpu.SemaphoreType.DMA
    patches, meta = pl.pallas_call(
        functools.partial(body, rows, pack, n_tm, n_dp, frame_counts.shape[1]),
        out_shape=(
            jax.ShapeDtypeStruct((n_dp, 2, block, 512), BF16),
            jax.ShapeDtypeStruct((n_dp, 8, wide), F32),
        ),
        in_specs=[anywhere, smem] + [vmem] * 9,
        out_specs=(anywhere, anywhere),
        scratch_shapes=[
            pltpu.VMEM((3, 2, HALF, 48, 128), BF16),
            pltpu.VMEM((6, HALF + 1, 48 + 2 * PAD, 128), F32),
            pltpu.VMEM((6, 14, 24 + 2 * PAD, 128), F32),
            pltpu.VMEM((2, 3, 1152, 256), BF16),
            pltpu.VMEM((2, 3, 1152, 256), BF16),
            pltpu.VMEM((PIECES, 240, 128), BF16),
            pltpu.VMEM((PIECES, 240, 128), BF16),
            pltpu.VMEM((2, 288, 128), F32),
            pltpu.VMEM((block, 512), F32),
            pltpu.VMEM((2, block, 512), BF16),
            pltpu.VMEM((block, 512), BF16),
            pltpu.VMEM((8, wide), F32),
            dma,
            dma((PIECES,)),
            dma((PIECES,)),
            dma((PIECES,)),
            dma((PIECES,)),
            dma((PIECES,)),
            dma((PIECES,)),
            dma,
            dma,
            dma((2, peers)),
            dma((2, peers)),
            dma((peers,)),
            dma((peers,)),
            dma((3,)),
        ],
        compiler_params=pltpu.CompilerParams(
            collective_id=0, has_side_effects=True, vmem_limit_bytes=56 * 1024 * 1024
        ),
        name="sections",
    )(
        features,
        frame_counts,
        conv1_weight.reshape(3, 1152, 128),
        conv1_bias.reshape(1, 128),
        shrink_weight,
        shrink_bias.reshape(1, 128),
        conv2_weight.reshape(3, 1152, 128),
        conv2_bias.reshape(1, 128),
        bucket_ids,
        dest_owner,
        dest_offset,
    )
    base = (lax.axis_index("dp") * pack + 1).astype(jnp.int32).reshape(1)
    tile = pack // 2
    packed = pl.pallas_call(
        functools.partial(embed, n_dp),
        grid=(pack // tile,),
        out_shape=jax.ShapeDtypeStruct((pack, lat), BF16),
        in_specs=[
            smem,
            pl.BlockSpec((n_dp, wide, 512), lambda i: (0, 0, 0)),
            pl.BlockSpec((n_dp, 8, wide), lambda i: (0, 0, 0)),
            pl.BlockSpec((512, lat), lambda i: (0, 0)),
            pl.BlockSpec((1, lat), lambda i: (0, 0)),
            pl.BlockSpec(bucket_table.shape, lambda i: (0, 0)),
        ],
        out_specs=pl.BlockSpec((tile, lat), lambda i: (i, 0)),
        compiler_params=pltpu.CompilerParams(vmem_limit_bytes=48 * 1024 * 1024),
        name="embed",
    )(
        base,
        patches.reshape(n_dp, wide, 512),
        meta,
        embed_weight,
        embed_bias.reshape(1, lat),
        bucket_table,
    )
    return packed[None]


def solution(mesh):
    sizes = dict(mesh.shape)
    return jax.shard_map(
        functools.partial(shards, sizes["dp"], sizes["tm"]),
        mesh=mesh,
        in_specs=(
            P("dp", "tm", None, None, None),
            P("dp", None),
            P(),
            P(),
            P(),
            P(),
            P(),
            P(),
            P(),
            P(),
            P(),
            P("dp", "tm"),
            P("dp", "tm"),
            P("dp", "tm"),
        ),
        out_specs=P("dp", "tm", None),
        check_vma=False,
    )
```
